512 devices in a mesh: section: 8 (over z_lo, core), dp: 64 (over z_hi, y, x).
Axes of the slice: x: 4, y: 8, z: 8 (z_hi: 2, z_lo: 4; z = z_hi * 4 + z_lo), core: 2. Of those that a mesh axis runs over, the one named last changes fastest.
Arguments:
- x_in: bfloat16 [8, 8192, 5120], P('section', 'dp'), may hold values from -8 to 8
- top_grad: bfloat16 [8192, 5120], P('dp'), may hold values from -6 to 6
- norm_gain: bfloat16 [8, 5120], P('section'), may hold values from 0.25 to 1.75
- proj_in: bfloat16 [8, 5120, 384], P('section', 'dp'), may hold values from -1 to 1
- proj_out: bfloat16 [8, 128, 5120], P('section', None, 'dp'), may hold values from -0.5 to 0.5
- key_cache: bfloat16 [8, 18432, 128], P('section', 'dp'), may hold values from -6 to 6
- value_cache: bfloat16 [8, 18432, 128], P('section', 'dp'), may hold values from -6 to 6
- prefix_len: int32 [64], P('dp'), may hold values from 72 to 288, as said below
- early_out: bfloat16 [8, 2048, 128], P('section', 'dp'), may hold values from -0.59765625 to 0.59765625
- early_dy: bfloat16 [8, 2048, 5120], P('section', 'dp'), may hold values from -16 to 16
Outputs:
- grad_x: bfloat16 [8, 8192, 5120], P('section', 'dp')
- key_cache_grad: bfloat16 [8, 18432, 128], P('section', 'dp')
- value_cache_grad: bfloat16 [8, 18432, 128], P('section', 'dp')
- wo_grad: float32 [8, 128, 5120], P('section', None, 'dp')
The draws below stay inside these ranges and needn't reach their ends.
Inputs may be any that keep to these rules, and one draw needn't show every extreme that they name: `prefix_len`: some sequence has all 288 cached positions.
All inputs are finite; a program needn't handle non-finite values.
Results may differ from the reference program's by a relative error of at most 0.02.
Values may be sent and summed in bfloat16 or wider, within the bound.
No kernel may reach another device: no remote copies, remote signals or barrier semaphores. Data moves between devices by JAX's collectives and lax.ppermute only.
A program may use at most 64 MiB of HBM per device.

```python
import jax
import jax.numpy as jnp
from jax import lax

D = 5120
HD = 128
TOK = 128
EROWS = 32
PREF = 288
LAYERS = 8
SEQS = 64


def weights_in(key):
    drawn = jax.random.normal(jax.random.fold_in(key, 101), (LAYERS, D, 3 * HD), jnp.float32)
    return jnp.clip(drawn, -6.0, 6.0) * D ** (-0.5)


def draw_proj_in(key, part):
    return weights_in(key).astype(jnp.bfloat16)


def draw_x_in(key, part):
    drawn = jnp.clip(jax.random.normal(jax.random.fold_in(key, 106), (LAYERS, SEQS, TOK, D), jnp.float32), -6.0, 6.0)
    return drawn.reshape(LAYERS, SEQS * TOK, D).astype(jnp.bfloat16)


def draw_key_cache(key, part):
    full_shape = (LAYERS, SEQS, PREF, HD)
    drawn = jnp.clip(jax.random.normal(jax.random.fold_in(key, 108), full_shape, jnp.float32), -6.0, 6.0)
    return drawn.reshape(LAYERS, SEQS * PREF, HD).astype(jnp.bfloat16)


def draw_prefix_len(key, part):
    lowest = max(8, PREF // 4)
    lengths = jax.random.randint(jax.random.fold_in(key, 109), (SEQS,), lowest, PREF + 1)
    fullest = jax.random.randint(jax.random.fold_in(key, 110), (), 0, SEQS)
    return jnp.where(jnp.arange(SEQS) == fullest, PREF, lengths).astype(jnp.int32)


def spiked(entries, stream_key, source, target, shards_of, factor):
    def block_of(dim):
        return (jnp.arange(entries.shape[dim]) // (entries.shape[dim] // shards_of)).reshape((-1,) + (1,) * (entries.ndim - 1 - dim))

    near = jax.random.permutation(stream_key, shards_of)[block_of(target)]
    far = (block_of(target) + shards_of // 2) % shards_of
    return jnp.where((block_of(source) == near) | (block_of(source) == far), factor * entries, entries)


def block_levels(stream_key, dims, split, smallest, largest):
    level = 1.0
    for axis_at, blocks in split:
        steps = jax.random.uniform(jax.random.fold_in(jax.random.fold_in(stream_key, 6), axis_at), (blocks,), jnp.float32, smallest / len(split), largest / len(split))
        level = level * jnp.repeat(jnp.exp(steps), dims[axis_at] // blocks).reshape((-1,) + (1,) * (len(dims) - 1 - axis_at))
    return level


def bell_draw(own_key, dims, scale, limit, shards=(), kind=jnp.bfloat16):
    entries = jax.random.normal(own_key, dims, jnp.float32) * scale
    if len(shards) > 0:
        entries = block_levels(own_key, dims, shards, -0.22, 0.18) * entries
    return jnp.clip(entries, min=-limit, max=limit).astype(kind)


def noise_with(own_key, shape, scale, bound, split, heavy, held_as=jnp.bfloat16):
    result = scale * jax.random.normal(own_key, shape, jnp.float32)
    if split:
        result = result * block_levels(own_key, shape, split, -0.22, 0.18)
    return jnp.clip(spiked(result, jax.random.fold_in(own_key, 3), *heavy), -bound, bound).astype(held_as)


def setup_inputs(seed: int = 0) -> dict:
    arg_keys = jax.random.split(jax.random.key(seed), 11)
    x_in = draw_x_in(jax.random.fold_in(arg_keys[10], 71), 0)
    top_grad = bell_draw(arg_keys[1], (SEQS * TOK, D), 1.0, 6.0, ((0, 64),))
    norm_gain = jnp.clip(1.0 + 0.15 * jax.random.normal(arg_keys[2], (LAYERS, D), jnp.float32), 0.25, 1.75).astype(jnp.bfloat16)
    proj_in = draw_proj_in(jax.random.fold_in(arg_keys[10], 71), 0)
    proj_out = bell_draw(arg_keys[4], (LAYERS, HD, D), HD ** -0.5, 0.5, ((0, 8), (2, 64)))
    key_cache = draw_key_cache(jax.random.fold_in(arg_keys[10], 71), 0)
    value_cache = bell_draw(arg_keys[6], (LAYERS, SEQS * PREF, HD), 1.0, 6.0, ((0, 8), (1, 64)))
    prefix_len = draw_prefix_len(jax.random.fold_in(arg_keys[10], 71), 0)
    early_out = bell_draw(arg_keys[8], (LAYERS, SEQS * EROWS, HD), 0.1, 0.59765625, ((0, 8), (1, 64)))
    early_dy = noise_with(arg_keys[9], (LAYERS, SEQS * EROWS, D), 1.0, 16.0, ((0, 8), (1, 64)), (1, 2, 64, 4.0))
    return dict(x_in=x_in, top_grad=top_grad, norm_gain=norm_gain, proj_in=proj_in, proj_out=proj_out, key_cache=key_cache, value_cache=value_cache, prefix_len=prefix_len, early_out=early_out, early_dy=early_dy)


eps = 1e-06

def layer_back(x_rows, grad_in, gain_row, proj_in, proj_out, cache_keys, cache_values, length):
    head_size = proj_out.shape[0]
    group_rows = x_rows.shape[0]
    cache_rows = cache_keys.shape[0]
    score_scale = head_size ** (-0.5)
    widened = x_rows.astype(jnp.float32)
    inv_rms = lax.rsqrt(lax.optimization_barrier(jnp.mean(widened * widened, axis=1, keepdims=True)) + eps)
    gain_wide = gain_row.astype(jnp.float32)
    normed = (widened * inv_rms * gain_wide).astype(jnp.bfloat16)
    projected = jnp.dot(normed, proj_in, preferred_element_type=jnp.float32).astype(jnp.bfloat16)
    queries = projected[:, :head_size]
    all_keys = jnp.concatenate([cache_keys, projected[:, head_size:2 * head_size]], axis=0)
    all_values = jnp.concatenate([cache_values, projected[:, 2 * head_size:]], axis=0)
    column = lax.broadcasted_iota(jnp.int32, (group_rows, cache_rows + group_rows), 1)
    position = lax.broadcasted_iota(jnp.int32, (group_rows, cache_rows + group_rows), 0)
    visible = jnp.where(column < cache_rows, column < length, column - cache_rows <= position)
    scores = jnp.dot(queries, all_keys.T, preferred_element_type=jnp.float32) * score_scale
    highest = lax.optimization_barrier(jnp.max(jnp.where(visible, scores, -jnp.inf), axis=1, keepdims=True))
    weights = jnp.where(visible, jnp.exp(scores - highest), 0.0)
    prob_full = weights / lax.optimization_barrier(jnp.sum(weights, axis=1, keepdims=True))
    prob_low = prob_full.astype(jnp.bfloat16)
    attended = jnp.dot(prob_low, all_values, preferred_element_type=jnp.float32).astype(jnp.bfloat16)
    grad_out = jnp.dot(grad_in, proj_out.T, preferred_element_type=jnp.float32).astype(jnp.bfloat16)
    grad_prob = jnp.dot(grad_out, all_values.T, preferred_element_type=jnp.float32)
    row_delta = lax.optimization_barrier(jnp.sum(prob_full * grad_prob, axis=1, keepdims=True))
    grad_score = (prob_full * (grad_prob - row_delta) * score_scale).astype(jnp.bfloat16)
    grad_query = jnp.dot(grad_score, all_keys, preferred_element_type=jnp.float32)
    grad_keys = jnp.dot(grad_score.T, queries, preferred_element_type=jnp.float32)
    grad_values = jnp.dot(prob_low.T, grad_out, preferred_element_type=jnp.float32)
    grad_proj = jnp.concatenate([grad_query, grad_keys[cache_rows:], grad_values[cache_rows:]], axis=1).astype(jnp.bfloat16)
    grad_norm = jnp.dot(grad_proj, proj_in.T, preferred_element_type=jnp.float32)
    scaled = grad_norm * gain_wide
    branch = inv_rms * scaled - widened * inv_rms * inv_rms * inv_rms * lax.optimization_barrier(jnp.mean(widened * scaled, axis=1, keepdims=True))
    grad_x = (grad_in.astype(jnp.float32) + branch).astype(jnp.bfloat16)
    return (grad_x, grad_keys[:cache_rows].astype(jnp.bfloat16), grad_values[:cache_rows].astype(jnp.bfloat16), attended)

def reference(x_in, top_grad, norm_gain, proj_in, proj_out, key_cache, value_cache, prefix_len, early_out, early_dy):
    x_all = x_in.reshape(LAYERS, SEQS, TOK, D)
    keys_all = key_cache.reshape(LAYERS, SEQS, PREF, HD)
    values_all = value_cache.reshape(LAYERS, SEQS, PREF, HD)
    grad_in = top_grad.reshape(SEQS, TOK, D)
    backward_all = jax.vmap(layer_back, in_axes=(0, 0, None, None, None, 0, 0, 0))
    grad_list = [None] * LAYERS
    key_list = [None] * LAYERS
    value_list = [None] * LAYERS
    wo_list = [None] * LAYERS
    for layer_num in reversed(range(LAYERS)):
        grad_x, key_grad, value_grad, attended = backward_all(x_all[layer_num], grad_in, norm_gain[layer_num], proj_in[layer_num], proj_out[layer_num], keys_all[layer_num], values_all[layer_num], prefix_len)
        current = jnp.dot(attended.reshape(SEQS * TOK, HD).T, grad_in.reshape(SEQS * TOK, D), preferred_element_type=jnp.float32)
        earlier = jnp.dot(early_out[layer_num].T, early_dy[layer_num], preferred_element_type=jnp.float32)
        grad_list[layer_num] = grad_x.reshape(SEQS * TOK, D)
        key_list[layer_num] = key_grad.reshape(SEQS * PREF, HD)
        value_list[layer_num] = value_grad.reshape(SEQS * PREF, HD)
        wo_list[layer_num] = current + earlier
        grad_in = grad_x
    return (jnp.stack(grad_list), jnp.stack(key_list), jnp.stack(value_list), jnp.stack(wo_list))
```

```python
import functools

import jax
import jax.numpy as jnp
from jax import lax
from jax.experimental import pallas as pl
from jax.experimental.pallas import tpu as pltpu
from jax.sharding import Mesh
from jax.sharding import PartitionSpec as P

eps = 1e-06
bf16 = jnp.bfloat16
f32 = jnp.float32
PARTS = 4
SECTION = ("zl", "core")
PLANE = ("y", "x")
DP = ("zh", "y", "x")
VMEM = pl.BlockSpec(memory_space=pltpu.VMEM)
ANY = pl.BlockSpec(memory_space=pl.ANY)
SMEM = pl.BlockSpec(memory_space=pltpu.SMEM)


def dot(a, b, ca=1, cb=0):
    return lax.dot_general(a, b, (((ca,), (cb,)), ((), ())), preferred_element_type=f32)


def chunk_of(width):
    return 640 if width % 640 == 0 else width


def forward_kernel(len_ref, normed, wg, kc, vc, q_ref, kn_ref, vn_ref, pc_ref, pn_ref, proj_ref, att_ref):
    half = wg.shape[0]
    hd = kc.shape[1]
    rows = normed.shape[0]
    step = chunk_of(half)
    acc = jnp.zeros((rows, 3 * hd), f32)
    for h in range(2):
        for c in range(0, half, step):
            acc = acc + dot(
                normed[:, h * half + c : h * half + c + step],
                wg[c : c + step, h * 4 * hd : h * 4 * hd + 3 * hd],
            )
    proj_ref[...] = acc
    low = acc.astype(bf16)
    q = low[:, :hd]
    kn = low[:, hd : 2 * hd]
    vn = low[:, 2 * hd :]
    q_ref[...] = q
    kn_ref[...] = kn
    vn_ref[...] = vn
    scale = hd ** (-0.5)
    sc = dot(q, kc[...], 1, 1) * scale
    sn = dot(q, kn, 1, 1) * scale
    see_c = lax.broadcasted_iota(jnp.int32, sc.shape, 1) < len_ref[0]
    see_n = lax.broadcasted_iota(jnp.int32, sn.shape, 1) <= lax.broadcasted_iota(jnp.int32, sn.shape, 0)
    sc = jnp.where(see_c, sc, -jnp.inf)
    sn = jnp.where(see_n, sn, -jnp.inf)
    top = jnp.maximum(jnp.max(sc, axis=1, keepdims=True), jnp.max(sn, axis=1, keepdims=True))
    wc = jnp.where(see_c, jnp.exp(sc - top), 0.0)
    wn = jnp.where(see_n, jnp.exp(sn - top), 0.0)
    total = jnp.sum(wc, axis=1, keepdims=True) + jnp.sum(wn, axis=1, keepdims=True)
    pc = wc / total
    pn = wn / total
    pc_ref[...] = pc
    pn_ref[...] = pn
    att_ref[...] = (dot(pc.astype(bf16), vc[...]) + dot(pn.astype(bf16), vn)).astype(bf16)


def stage_kernel(
    flags, recv, top, wg, x, gain, inv, q, kc, kn, vc, vn, pc, pn, proj, gkn_in, gvn_in, gsc_in, go_in,
    send, gkn, gvn, gsc, go_all, gin, wo_buf, wi_buf, x_buf, gin_sem, wo_sem, wi_sem, x_sem,
):
    rows = send.shape[0]
    hd = q.shape[1]
    half = wg.shape[0]
    step = chunk_of(half)
    scale = hd ** (-0.5)
    active = flags[0] == 1
    r0 = pl.multiple_of(flags[1] * rows, rows)
    is_top = flags[2] == 1
    mine = pl.ds(r0, rows)
    pieces = [(h, c) for h in range(2) for c in range(0, half, step)]
    take_top = pltpu.make_async_copy(top.at[mine, :], gin, gin_sem)
    take_recv = pltpu.make_async_copy(recv, gin, gin_sem)
    take_x = pltpu.make_async_copy(x.at[mine, :], x_buf, x_sem)
    take_wo = []
    take_wi = []
    for n, (h, c) in enumerate(pieces):
        take_wo.append(
            pltpu.make_async_copy(
                wg.at[pl.ds(c, step), pl.ds(h * 4 * hd + 3 * hd, hd)],
                wo_buf.at[pl.ds(n * step, step), :],
                wo_sem.at[n],
            )
        )
        take_wi.append(
            pltpu.make_async_copy(
                wg.at[pl.ds(c, step), pl.ds(h * 4 * hd, 3 * hd)],
                wi_buf.at[pl.ds(n * step, step), :],
                wi_sem.at[n],
            )
        )

    @pl.when(jnp.logical_and(active, is_top))
    def _():
        take_top.start()

    @pl.when(jnp.logical_and(active, jnp.logical_not(is_top)))
    def _():
        take_recv.start()

    @pl.when(active)
    def _():
        for copy in take_wo:
            copy.start()
        for copy in take_wi:
            copy.start()
        take_x.start()

    gkn[...] = gkn_in[...]
    gvn[...] = gvn_in[...]
    gsc[...] = gsc_in[...]
    go_all[...] = go_in[...]

    @pl.when(active)
    def _():
        take_recv.wait()
        acc = jnp.zeros((rows, hd), f32)
        for n in range(len(pieces)):
            take_wo[n].wait()
            acc = acc + dot(gin[:, n * step : (n + 1) * step], wo_buf[n * step : (n + 1) * step, :])
        go = acc.astype(bf16)
        go_all[mine, :] = go
        prob_c = pc[mine, :]
        prob_n = pn[mine, :]
        gp_c = dot(go, vc[...], 1, 1)
        gp_n = dot(go, vn[...], 1, 1)
        delta = jnp.sum(prob_c * gp_c, axis=1, keepdims=True) + jnp.sum(prob_n * gp_n, axis=1, keepdims=True)
        gs_c = (prob_c * (gp_c - delta) * scale).astype(bf16)
        gs_n = (prob_n * (gp_n - delta) * scale).astype(bf16)
        gsc[mine, :] = gs_c
        gq = dot(gs_c, kc[...]) + dot(gs_n, kn[...])
        gkn[...] += dot(gs_n, q[mine, :], 0, 0)
        gvn[...] += dot(prob_n.astype(bf16), go, 0, 0)
        gproj = jnp.concatenate([gq, gkn[mine, :], gvn[mine, :]], axis=1).astype(bf16)
        r = inv[mine, :]
        coef = r * r * jnp.sum(gproj.astype(f32) * proj[mine, :], axis=1, keepdims=True) * (1.0 / (2 * half))
        take_x.wait()
        for n in range(len(pieces)):
            cols = slice(n * step, (n + 1) * step)
            take_wi[n].wait()
            gn = dot(gproj, wi_buf[cols, :], 1, 1)
            out = gin[:, cols].astype(f32) + r * (gn * gain[:, cols]) - x_buf[:, cols].astype(f32) * coef
            send[:, cols] = out.astype(bf16)


def turn_kernel(gin, out):
    tokens, width = gin.shape
    planes = out.shape[0]
    shard = out.shape[1] // 2
    flipped = jnp.transpose(gin[...].astype(f32)).astype(bf16)
    for h in range(2):
        for p in range(planes):
            base = (h * planes + p) * shard
            out[p, h * shard : (h + 1) * shard, :] = flipped[base : base + shard, :]


def contract_kernel(got, att, early, out):
    planes, wide, tokens = got.shape
    acc = early[...]
    for p in range(0, planes, 2):
        lhs = jnp.concatenate([got[p], got[p + 1]], axis=1)
        rhs = jnp.concatenate([att[p, :tokens, :], att[p + 1, :tokens, :]], axis=0)
        acc = acc + dot(lhs, rhs)
    out[...] = acc


def body(x_in, top_grad, norm_gain, proj_in, proj_out, key_cache, value_cache, prefix_len, early_out, early_dy):
    sections = lax.axis_size(SECTION)
    section = lax.axis_index(SECTION)
    zh = lax.axis_index("zh")
    planes = lax.axis_size(PLANE)
    x = x_in[0]
    tokens, width = x.shape
    kc = key_cache[0]
    vc = value_cache[0]
    crow, hd = kc.shape
    shard = width // (2 * planes)
    erows = early_dy.shape[1]
    swap = [(0, 1), (1, 0)]

    with jax.named_scope("weights"):
        own = jnp.concatenate([proj_in[0], jnp.transpose(proj_out[0])], axis=1)
        other = lax.ppermute(own, "zh", swap)
        pair = jnp.where(
            zh == 0, jnp.concatenate([own, other], axis=1), jnp.concatenate([other, own], axis=1)
        )
        wg = lax.all_gather(pair, PLANE, axis=0, tiled=True)

    with jax.named_scope("early"):
        packed = early_dy[0].reshape(erows, 2, planes, 2, shard // 2)
        packed = packed.transpose(2, 4, 1, 3, 0).reshape(planes, shard // 2, 4 * erows)
        early_got = lax.all_to_all(packed, PLANE, 0, 0, tiled=True)

    with jax.named_scope("norm"):
        wide = x.astype(f32)
        gain = norm_gain.astype(f32)
        inv = lax.rsqrt(jnp.mean(wide * wide, axis=1, keepdims=True) + eps)
        normed = (wide * inv * gain).astype(bf16)

    shape = jax.ShapeDtypeStruct
    q, kn, vn, pc, pn, proj, att = pl.pallas_call(
        forward_kernel,
        name="forward",
        in_specs=[SMEM, VMEM, VMEM, VMEM, VMEM],
        out_specs=[VMEM] * 7,
        out_shape=[
            shape((tokens, hd), bf16),
            shape((tokens, hd), bf16),
            shape((tokens, hd), bf16),
            shape((tokens, crow), f32),
            shape((tokens, tokens), f32),
            shape((tokens, 3 * hd), f32),
            shape((tokens, hd), bf16),
        ],
        compiler_params=pltpu.CompilerParams(vmem_limit_bytes=24 << 20),
    )(prefix_len, normed, wg, kc, vc)

    with jax.named_scope("attended"):
        att_all = lax.all_gather(jnp.concatenate([att, early_out[0]], axis=0)[None], PLANE, axis=0, tiled=True)

    rows = tokens // PARTS
    copies = width // chunk_of(width // 2)
    stage = pl.pallas_call(
        stage_kernel,
        name="stage",
        in_specs=[SMEM] + [ANY] * 4 + [VMEM] * 14,
        out_specs=[VMEM] * 5,
        out_shape=[
            shape((rows, width), bf16),
            shape((tokens, hd), f32),
            shape((tokens, hd), f32),
            shape((tokens, crow), bf16),
            shape((tokens, hd), bf16),
        ],
        scratch_shapes=[
            pltpu.VMEM((rows, width), bf16),
            pltpu.VMEM((width, hd), bf16),
            pltpu.VMEM((width, 3 * hd), bf16),
            pltpu.VMEM((rows, width), bf16),
            pltpu.SemaphoreType.DMA,
            pltpu.SemaphoreType.DMA((copies,)),
            pltpu.SemaphoreType.DMA((copies,)),
            pltpu.SemaphoreType.DMA,
        ],
        input_output_aliases={15: 1, 16: 2, 17: 3, 18: 4},
        compiler_params=pltpu.CompilerParams(vmem_limit_bytes=24 << 20),
    )
    is_top = section == sections - 1

    def place(t):
        part = sections - 1 - section + PARTS - 1 - t
        active = jnp.logical_and(part >= 0, part < PARTS)
        return jnp.clip(part, 0, PARTS - 1), active

    def keep(whole, piece, t, also):
        part, active = place(t)
        at = part * rows
        old = lax.dynamic_slice_in_dim(whole, at, rows, 0)
        return lax.dynamic_update_slice_in_dim(
            whole, jnp.where(jnp.logical_and(active, also), piece, old), at, 0
        )

    def compute(t, recv, state):
        part, active = place(t)
        flags = jnp.stack([active.astype(jnp.int32), part, is_top.astype(jnp.int32)])
        return stage(flags, recv, top_grad, wg, x, gain, inv, q, kc, kn, vc, vn, pc, pn, proj, *state)

    def one_turn(t, carried):
        recv, gin_all, gx_all, state = carried
        send, *state = compute(t, recv, state)
        passed = lax.ppermute(send, SECTION, [(i, i - 1) for i in range(1, sections)])
        gin_all = keep(gin_all, recv, t, jnp.logical_not(is_top))
        gx_all = keep(gx_all, send, t, True)
        return passed, gin_all, gx_all, tuple(state)

    carried = (
        jnp.zeros((rows, width), bf16),
        jnp.where(is_top, top_grad, jnp.zeros_like(top_grad)),
        jnp.zeros((tokens, width), bf16),
        (
            jnp.zeros((tokens, hd), f32),
            jnp.zeros((tokens, hd), f32),
            jnp.zeros((tokens, crow), bf16),
            jnp.zeros((tokens, hd), bf16),
        ),
    )
    turns = sections + PARTS - 1
    recv, gin_all, gx_all, state = lax.fori_loop(0, turns - 1, one_turn, carried)
    gin_all = keep(gin_all, recv, turns - 1, jnp.logical_not(is_top))
    with jax.named_scope("owners"):
        turned = pl.pallas_call(
            turn_kernel,
            name="turn",
            in_specs=[VMEM],
            out_specs=VMEM,
            out_shape=shape((planes, 2 * shard, tokens), bf16),
            compiler_params=pltpu.CompilerParams(vmem_limit_bytes=24 << 20),
        )(gin_all)
        got = lax.all_to_all(turned, PLANE, 0, 0, tiled=True)
    send, gkn, gvn, gsc, go_all = compute(turns - 1, recv, state)
    gx_all = keep(gx_all, send, turns - 1, True)
    with jax.named_scope("cache"):
        key_out = dot(gsc, q, 0, 0).astype(bf16)
        value_out = dot(pc.astype(bf16), go_all, 0, 0).astype(bf16)
    with jax.named_scope("early_sum"):
        early_rows = early_got.reshape(planes, shard // 2, 4, erows)
        early = jnp.einsum("prqt,pth->qrh", early_rows, att_all[:, tokens:, :], preferred_element_type=f32)
        early = early.reshape(2 * shard, hd)
    with jax.named_scope("sum"):
        whole = pl.pallas_call(
            contract_kernel,
            name="contract",
            in_specs=[VMEM] * 3,
            out_specs=VMEM,
            out_shape=shape((2 * shard, hd), f32),
            compiler_params=pltpu.CompilerParams(vmem_limit_bytes=24 << 20),
        )(got, att_all, early)
        first, second = whole[:shard], whole[shard:]
        away = lax.ppermute(jnp.where(zh == 0, second, first), "zh", swap)
        wo = jnp.transpose(jnp.where(zh == 0, first, second) + away)
    return gx_all[None], key_out[None], value_out[None], wo[None]


def solution(mesh):
    ny, nx = (8, 4) if mesh.shape["dp"] == 64 else (2, mesh.shape["dp"] // 4)
    fine = Mesh(mesh.devices.reshape(mesh.shape["section"] // 2, 2, 2, ny, nx), ("zl", "core", "zh", "y", "x"))
    in_specs = (
        P(SECTION, DP, None),
        P(DP, None),
        P(SECTION, None),
        P(SECTION, DP, None),
        P(SECTION, None, DP),
        P(SECTION, DP, None),
        P(SECTION, DP, None),
        P(DP),
        P(SECTION, DP, None),
        P(SECTION, DP, None),
    )
    out_specs = (
        P(SECTION, DP, None),
        P(SECTION, DP, None),
        P(SECTION, DP, None),
        P(SECTION, None, DP),
    )
    return jax.shard_map(body, mesh=fine, in_specs=in_specs, out_specs=out_specs, check_vma=False)
```

```python
import functools

import jax
import jax.numpy as jnp
from jax import lax
from jax.experimental import pallas as pl
from jax.experimental.pallas import tpu as pltpu
from jax.sharding import Mesh
from jax.sharding import PartitionSpec as P


eps = 1e-06
bf16 = jnp.bfloat16
f32 = jnp.float32
PARTS = 4
SECTION = ("zl", "core")
PLANE = ("y", "x")
DP = ("zh", "y", "x")
VMEM = pl.BlockSpec(memory_space=pltpu.VMEM)
ANY = pl.BlockSpec(memory_space=pl.ANY)
SMEM = pl.BlockSpec(memory_space=pltpu.SMEM)


def dot(a, b, ca=1, cb=0):
    return lax.dot_general(a, b, (((ca,), (cb,)), ((), ())), preferred_element_type=f32)


def near(a):
    return pltpu.with_memory_space_constraint(a, pltpu.VMEM)


def chunk_of(width):
    return 640 if width % 640 == 0 else width


def forward_kernel(
    len_ref, normed, wa, wb, kc, vc, eo, w, q_ref, kn_ref, vn_ref, pc_ref, pn_ref, proj_ref, att_ref, sem_a, sem_b,
):
    hd = kc.shape[1]
    rows = normed.shape[0]
    nx, ny, shard, _ = wb.shape
    half = nx * ny * shard
    step = chunk_of(half)
    take_a = [
        pltpu.make_async_copy(
            wa.at[p // nx, lax.rem(len_ref[1] - p % nx + nx, nx)], w.at[pl.ds(p * shard, shard), :], sem_a.at[p]
        )
        for p in range(nx * ny)
    ]
    take_b = [
        pltpu.make_async_copy(wb.at[p % nx, p // nx], w.at[pl.ds(half + p * shard, shard), :], sem_b.at[p])
        for p in range(nx * ny)
    ]
    for copy in take_a + take_b:
        copy.start()
    acc = jnp.zeros((rows, 3 * hd), f32)
    for h in range(2):
        for c in range(0, half, step):
            for p in range(c // shard, (c + step) // shard):
                (take_a, take_b)[h][p].wait()
            at = h * half + c
            acc = acc + dot(normed[:, at : at + step], w[at : at + step, : 3 * hd])
    proj_ref[...] = acc
    low = acc.astype(bf16)
    q = low[:, :hd]
    kn = low[:, hd : 2 * hd]
    vn = low[:, 2 * hd :]
    q_ref[...] = q
    kn_ref[...] = kn
    vn_ref[...] = vn
    scale = hd ** (-0.5)
    sc = dot(q, kc[...], 1, 1) * scale
    sn = dot(q, kn, 1, 1) * scale
    see_c = lax.broadcasted_iota(jnp.int32, sc.shape, 1) < len_ref[0]
    see_n = lax.broadcasted_iota(jnp.int32, sn.shape, 1) <= lax.broadcasted_iota(jnp.int32, sn.shape, 0)
    sc = jnp.where(see_c, sc, -jnp.inf)
    sn = jnp.where(see_n, sn, -jnp.inf)
    top = jnp.maximum(jnp.max(sc, axis=1, keepdims=True), jnp.max(sn, axis=1, keepdims=True))
    wc = jnp.where(see_c, jnp.exp(sc - top), 0.0)
    wn = jnp.where(see_n, jnp.exp(sn - top), 0.0)
    total = jnp.sum(wc, axis=1, keepdims=True) + jnp.sum(wn, axis=1, keepdims=True)
    pc = wc / total
    pn = wn / total
    pc_ref[...] = pc
    pn_ref[...] = pn
    att_ref[:rows, :] = (dot(pc.astype(bf16), vc[...]) + dot(pn.astype(bf16), vn)).astype(bf16)
    att_ref[rows:, :] = eo[...]


def stage_kernel(
    flags, recv, top, w, x, gain, inv, q, kc, kn, vc, vn, pc, pn, proj, gkn_in, gvn_in, gsc_in, go_in,
    send, gkn, gvn, gsc, go_all, gin,
):
    rows = send.shape[0]
    hd = q.shape[1]
    width = w.shape[0]
    step = chunk_of(width // 2)
    scale = hd ** (-0.5)
    active = flags[0] == 1
    r0 = pl.multiple_of(flags[1] * rows, rows)
    is_top = flags[2] == 1
    mine = pl.ds(r0, rows)
    pieces = [slice(c, c + step) for c in range(0, width, step)]

    gkn[...] = gkn_in[...]
    gvn[...] = gvn_in[...]
    gsc[...] = gsc_in[...]
    go_all[...] = go_in[...]

    @pl.when(jnp.logical_and(active, is_top))
    def _():
        gin[...] = top[mine, :]

    @pl.when(jnp.logical_and(active, jnp.logical_not(is_top)))
    def _():
        gin[...] = recv[...]

    @pl.when(active)
    def _():
        acc = jnp.zeros((rows, hd), f32)
        for cols in pieces:
            acc = acc + dot(gin[:, cols], w[cols, 3 * hd :])
        go = acc.astype(bf16)
        go_all[mine, :] = go
        prob_c = pc[mine, :]
        prob_n = pn[mine, :]
        gp_c = dot(go, vc[...], 1, 1)
        gp_n = dot(go, vn[...], 1, 1)
        delta = jnp.sum(prob_c * gp_c, axis=1, keepdims=True) + jnp.sum(prob_n * gp_n, axis=1, keepdims=True)
        gs_c = (prob_c * (gp_c - delta) * scale).astype(bf16)
        gs_n = (prob_n * (gp_n - delta) * scale).astype(bf16)
        gsc[mine, :] = gs_c
        gq = dot(gs_c, kc[...]) + dot(gs_n, kn[...])
        gkn[...] += dot(gs_n, q[mine, :], 0, 0)
        gvn[...] += dot(prob_n.astype(bf16), go, 0, 0)
        gproj = jnp.concatenate([gq, gkn[mine, :], gvn[mine, :]], axis=1).astype(bf16)
        r = inv[mine, :]
        coef = r * r * jnp.sum(gproj.astype(f32) * proj[mine, :], axis=1, keepdims=True) * (1.0 / width)

        @pl.loop(0, width // step)
        def _(n):
            cols = pl.ds(pl.multiple_of(n * step, step), step)
            gn = dot(gproj, w[cols, : 3 * hd], 1, 1)
            out = gin[:, cols].astype(f32) + r * (gn * gain[:, cols]) - x[mine, cols].astype(f32) * coef
            send[:, cols] = out.astype(bf16)


def flip(block, out):
    planes, shard, _ = out.shape
    half = planes * shard
    pair = jnp.concatenate([block[:, :half], block[:, half:]], axis=0)
    turned = jnp.transpose(pair.astype(f32)).astype(bf16)
    for p in range(planes):
        out[p] = turned[p * shard : (p + 1) * shard, :]


def turn_early_half(gin, out):
    tokens = gin.shape[0]
    flip(gin[tokens // 2 :, :], out)


def turn_late_half(flag, gin, recv, out):
    tokens = gin.shape[0]
    rows = recv.shape[0]
    first = jnp.where(flag[0] == 1, recv[...], gin[:rows, :])
    flip(jnp.concatenate([first, gin[rows : tokens // 2, :]], axis=0), out)


def contract_kernel(start, got, att, sofar, out):
    planes, _, tokens = got.shape
    tokens = tokens // 2
    hd = att.shape[2]
    acc = sofar[...]
    none = jnp.zeros((tokens, hd), bf16)
    for p in range(0, planes, 2):
        lhs = jnp.concatenate([got[p], got[p + 1]], axis=1)
        rhs = []
        for b in (p, p + 1):
            a = att[b, start : start + tokens, :]
            rhs += [jnp.concatenate([a, none], axis=1), jnp.concatenate([none, a], axis=1)]
        acc = acc + dot(lhs, jnp.concatenate(rhs, axis=0))
    out[...] = acc


def body(x_in, top_grad, norm_gain, proj_in, proj_out, key_cache, value_cache, prefix_len, early_out, early_dy):
    sections = lax.axis_size(SECTION)
    section = lax.axis_index(SECTION)
    zh = lax.axis_index("zh")
    planes = lax.axis_size(PLANE)
    x = x_in[0]
    tokens, width = x.shape
    kc = key_cache[0]
    vc = value_cache[0]
    crow, hd = kc.shape
    shard = width // (2 * planes)
    erows = early_dy.shape[1]
    swap = [(0, 1), (1, 0)]

    own = jnp.concatenate([proj_in[0], jnp.transpose(proj_out[0])], axis=1)
    other = lax.ppermute(own, "zh", swap)
    lower = jnp.where(zh == 0, own, other)
    upper = jnp.where(zh == 0, other, own)
    nx = lax.axis_size("x")
    ny = lax.axis_size("y")
    along_y = lax.all_to_all(jnp.broadcast_to(upper[None], (ny, *upper.shape)), "y", 0, 0, tiled=True)
    turns_x = [lower] + [lax.ppermute(lower, "x", [(i, (i + d) % nx) for i in range(nx)]) for d in range(1, nx)]
    wa = lax.all_gather(jnp.stack(turns_x)[None], "y", axis=0, tiled=True)
    wb = lax.all_to_all(jnp.broadcast_to(along_y[None], (nx, *along_y.shape)), "x", 0, 0, tiled=True)

    wide = x.astype(f32)
    gain = norm_gain.astype(f32)
    inv = lax.rsqrt(jnp.mean(wide * wide, axis=1, keepdims=True) + eps)
    normed = (wide * inv * gain).astype(bf16)

    packed = early_dy[0].reshape(erows, 2, planes, 2, shard // 2)
    packed = packed.transpose(2, 4, 1, 3, 0).reshape(planes, shard // 2, 4 * erows)

    shape = jax.ShapeDtypeStruct
    room = pltpu.CompilerParams(vmem_limit_bytes=24 << 20)
    w, q, kn, vn, pc, pn, proj, att = pl.pallas_call(
        forward_kernel,
        name="forward",
        in_specs=[SMEM, VMEM, ANY, ANY, VMEM, VMEM, VMEM],
        out_specs=[VMEM] * 8,
        out_shape=[
            shape((width, 4 * hd), bf16),
            shape((tokens, hd), bf16),
            shape((tokens, hd), bf16),
            shape((tokens, hd), bf16),
            shape((tokens, crow), f32),
            shape((tokens, tokens), f32),
            shape((tokens, 3 * hd), f32),
            shape((tokens + erows, hd), bf16),
        ],
        scratch_shapes=[
            pltpu.SemaphoreType.DMA((planes,)),
            pltpu.SemaphoreType.DMA((planes,)),
        ],
        compiler_params=room,
    )(jnp.stack([prefix_len[0], lax.axis_index("x")]), normed, wa, wb, kc, vc, early_out[0])
    w = near(w)

    att_all = lax.all_gather(att[None], PLANE, axis=0, tiled=True)

    rows = tokens // PARTS
    stage = pl.pallas_call(
        stage_kernel,
        name="stage",
        in_specs=[SMEM] + [VMEM] * 18,
        out_specs=[VMEM] * 5,
        out_shape=[
            shape((rows, width), bf16),
            shape((tokens, hd), f32),
            shape((tokens, hd), f32),
            shape((tokens, crow), bf16),
            shape((tokens, hd), bf16),
        ],
        scratch_shapes=[pltpu.VMEM((rows, width), bf16)],
        input_output_aliases={15: 1, 16: 2, 17: 3, 18: 4},
        compiler_params=room,
    )
    is_top = section == sections - 1

    def place(t):
        part = sections - 1 - section + PARTS - 1 - t
        active = jnp.logical_and(part >= 0, part < PARTS)
        return jnp.clip(part, 0, PARTS - 1), active

    def keep(whole, piece, t, also):
        part, active = place(t)
        at = part * rows
        old = lax.dynamic_slice_in_dim(whole, at, rows, 0)
        return lax.dynamic_update_slice_in_dim(
            whole, jnp.where(jnp.logical_and(active, also), piece, old), at, 0
        )

    def compute(t, recv, state):
        part, active = place(t)
        flags = jnp.stack([active.astype(jnp.int32), part, is_top.astype(jnp.int32)])
        return stage(flags, recv, top_grad, w, x, gain, inv, q, kc, kn, vc, vn, pc, pn, proj, *state)

    packed, _ = lax.optimization_barrier((packed, att))
    early_got = lax.all_to_all(packed, PLANE, 0, 0, tiled=True)

    recv = jnp.zeros((rows, width), bf16)
    gin_all = jnp.where(is_top, top_grad, jnp.zeros_like(top_grad))
    gx_all = jnp.zeros((tokens, width), bf16)
    state = (
        jnp.zeros((tokens, hd), f32),
        jnp.zeros((tokens, hd), f32),
        jnp.zeros((tokens, crow), bf16),
        jnp.zeros((tokens, hd), bf16),
    )
    turns = sections + PARTS - 1
    block = shape((planes, shard, tokens), bf16)
    down = [(i, i - 1) for i in range(1, sections)]

    halfway = sections + PARTS // 2 - 2
    for t in range(turns):
        if t == turns - 1:
            flag = (section == 0).astype(jnp.int32)[None]
            late = pl.pallas_call(
                turn_late_half,
                name="turn_late",
                in_specs=[SMEM, VMEM, VMEM],
                out_specs=VMEM,
                out_shape=block,
                compiler_params=room,
            )(flag, gin_all, recv)
            recv, late, got_soon = lax.optimization_barrier((recv, late, got_soon))
            got_late = lax.all_to_all(late, PLANE, 0, 0, tiled=True)
        elif t > 0:
            gin_all = keep(gin_all, recv, t, jnp.logical_not(is_top))
        send, *state = compute(t, recv, state)
        gx_all = keep(gx_all, send, t, True)
        if t == halfway:
            gin_now, _, early_got = lax.optimization_barrier((gin_all, send, early_got))
            soon = pl.pallas_call(
                turn_early_half,
                name="turn_soon",
                in_specs=[VMEM],
                out_specs=VMEM,
                out_shape=block,
                compiler_params=room,
            )(gin_now)
            got_soon = lax.all_to_all(soon, PLANE, 0, 0, tiled=True)
        if t < turns - 1:
            recv = lax.ppermute(send, SECTION, down)
    _, _, gsc, go_all = state
    key_out = dot(gsc, q, 0, 0).astype(bf16)
    value_out = dot(pc.astype(bf16), go_all, 0, 0).astype(bf16)
    early_got, _ = lax.optimization_barrier((early_got, send))
    early_rows = early_got.reshape(planes, shard // 2, 4, erows)
    early = jnp.einsum("prqt,pth->qrh", early_rows, att_all[:, tokens:, :], preferred_element_type=f32)
    early = early.reshape(2, shard, hd)
    early = jnp.concatenate([early[0], early[1]], axis=1)

    def contract(start, got, sofar):
        return pl.pallas_call(
            functools.partial(contract_kernel, start),
            name="contract",
            in_specs=[VMEM] * 3,
            out_specs=VMEM,
            out_shape=shape((shard, 2 * hd), f32),
            compiler_params=room,
        )(got, att_all, sofar)

    whole = contract(tokens // 2, got_soon, early)
    whole = contract(0, got_late, whole)
    first, second = whole[:, :hd], whole[:, hd:]
    away = lax.ppermute(jnp.where(zh == 0, second, first), "zh", swap)
    wo = jnp.transpose(jnp.where(zh == 0, first, second) + away)
    return gx_all[None], key_out[None], value_out[None], wo[None]


def solution(mesh):
    ny, nx = (8, 4) if mesh.shape["dp"] == 64 else (2, mesh.shape["dp"] // 4)
    fine = Mesh(mesh.devices.reshape(mesh.shape["section"] // 2, 2, 2, ny, nx), ("zl", "core", "zh", "y", "x"))
    in_specs = (
        P(SECTION, DP, None),
        P(DP, None),
        P(SECTION, None),
        P(SECTION, DP, None),
        P(SECTION, None, DP),
        P(SECTION, DP, None),
        P(SECTION, DP, None),
        P(DP),
        P(SECTION, DP, None),
        P(SECTION, DP, None),
    )
    out_specs = (
        P(SECTION, DP, None),
        P(SECTION, DP, None),
        P(SECTION, DP, None),
        P(SECTION, None, DP),
    )
    return jax.shard_map(body, mesh=fine, in_specs=in_specs, out_specs=out_specs, check_vma=False)
```

```python
import jax
import jax.numpy as jnp
from jax import lax
from jax.experimental import pallas as pl
from jax.experimental.pallas import tpu as pltpu
from jax.sharding import Mesh
from jax.sharding import PartitionSpec as P


eps = 1e-06
bf16 = jnp.bfloat16
f32 = jnp.float32
PARTS = 4
SECTION = ("zl", "core")
PLANE = ("y", "x")
DP = ("zh", "y", "x")
VMEM = pl.BlockSpec(memory_space=pltpu.VMEM)
HBM = pl.BlockSpec(memory_space=pltpu.HBM)
SMEM = pl.BlockSpec(memory_space=pltpu.SMEM)


def dot(a, b, ca=1, cb=0):
    return lax.dot_general(a, b, (((ca,), (cb,)), ((), ())), preferred_element_type=f32)


def near(a):
    return pltpu.with_memory_space_constraint(a, pltpu.VMEM)


def chunk_of(width):
    return 640 if width % 640 == 0 else width


def forward_kernel(
    place, normed_hbm, wa, wb, kc, vc, eo, w, q_ref, kn_ref, vn_ref, pc_ref, pn_ref, proj_ref, att_ref,
    normed, sem_a, sem_b, sem_n,
):
    len_ref = place
    hd = kc.shape[1]
    rows, width = normed.shape
    nx, ny, shard, _ = wb.shape
    half = width // 2
    zh = place[2]
    take_a = [
        pltpu.make_async_copy(wa.at[:, lax.rem(place[1] - j + nx, nx)], w.at[zh, :, j], sem_a.at[j]) for j in range(nx)
    ]
    take_b = [pltpu.make_async_copy(wb.at[j], w.at[1 - zh, :, j], sem_b.at[j]) for j in range(nx)]
    take_n = pltpu.make_async_copy(normed_hbm, normed, sem_n)
    take_n.start()
    for copy in take_a + take_b:
        copy.start()
    take_n.wait()
    acc = jnp.zeros((rows, 3 * hd), f32)
    deep = max(1, ny // 4)
    step = deep * nx * shard
    for h, copies in ((zh, take_a), (1 - zh, take_b)):
        for copy in copies:
            copy.wait()
        for c in range(0, ny, deep):
            cols = pl.ds(pl.multiple_of(h * half + c * nx * shard, 128), step)
            acc = acc + dot(normed[:, cols], w[h, c : c + deep, :, :, : 3 * hd].reshape(step, 3 * hd))
    proj_ref[...] = acc
    low = acc.astype(bf16)
    q = low[:, :hd]
    kn = low[:, hd : 2 * hd]
    vn = low[:, 2 * hd :]
    q_ref[...] = q
    kn_ref[...] = kn
    vn_ref[...] = vn
    scale = hd ** (-0.5)
    sc = dot(q, kc[...], 1, 1) * scale
    sn = dot(q, kn, 1, 1) * scale
    see_c = lax.broadcasted_iota(jnp.int32, sc.shape, 1) < len_ref[0]
    see_n = lax.broadcasted_iota(jnp.int32, sn.shape, 1) <= lax.broadcasted_iota(jnp.int32, sn.shape, 0)
    sc = jnp.where(see_c, sc, -jnp.inf)
    sn = jnp.where(see_n, sn, -jnp.inf)
    top = jnp.maximum(jnp.max(sc, axis=1, keepdims=True), jnp.max(sn, axis=1, keepdims=True))
    wc = jnp.where(see_c, jnp.exp(sc - top), 0.0)
    wn = jnp.where(see_n, jnp.exp(sn - top), 0.0)
    total = jnp.sum(wc, axis=1, keepdims=True) + jnp.sum(wn, axis=1, keepdims=True)
    pc = wc / total
    pn = wn / total
    pc_ref[...] = pc
    pn_ref[...] = pn
    att_ref[:rows, :] = (dot(pc.astype(bf16), vc[...]) + dot(pn.astype(bf16), vn)).astype(bf16)
    att_ref[rows:, :] = eo[...]


def stage_kernel(
    flags, recv, top, w, x, gain, inv, q, kc, kn, vc, vn, pc, pn, proj, gkn_in, gvn_in, gsc_in, go_in,
    send, gkn, gvn, gsc, go_all, gin,
):
    rows = send.shape[0]
    hd = q.shape[1]
    width = w.shape[0]
    step = chunk_of(width // 2)
    scale = hd ** (-0.5)
    active = flags[0] == 1
    r0 = pl.multiple_of(flags[1] * rows, rows)
    is_top = flags[2] == 1
    mine = pl.ds(r0, rows)
    pieces = [slice(c, c + step) for c in range(0, width, step)]

    gkn[...] = gkn_in[...]
    gvn[...] = gvn_in[...]
    gsc[...] = gsc_in[...]
    go_all[...] = go_in[...]

    @pl.when(jnp.logical_and(active, is_top))
    def _():
        gin[...] = top[mine, :]

    @pl.when(jnp.logical_and(active, jnp.logical_not(is_top)))
    def _():
        gin[...] = recv[...]

    @pl.when(active)
    def _():
        acc = jnp.zeros((rows, hd), f32)
        for cols in pieces:
            acc = acc + dot(gin[:, cols], w[cols, 3 * hd :])
        go = acc.astype(bf16)
        go_all[mine, :] = go
        prob_c = pc[mine, :]
        prob_n = pn[mine, :]
        gp_c = dot(go, vc[...], 1, 1)
        gp_n = dot(go, vn[...], 1, 1)
        delta = jnp.sum(prob_c * gp_c, axis=1, keepdims=True) + jnp.sum(prob_n * gp_n, axis=1, keepdims=True)
        gs_c = (prob_c * (gp_c - delta) * scale).astype(bf16)
        gs_n = (prob_n * (gp_n - delta) * scale).astype(bf16)
        gsc[mine, :] = gs_c
        gq = dot(gs_c, kc[...]) + dot(gs_n, kn[...])
        gkn[...] += dot(gs_n, q[mine, :], 0, 0)
        gvn[...] += dot(prob_n.astype(bf16), go, 0, 0)
        gproj = jnp.concatenate([gq, gkn[mine, :], gvn[mine, :]], axis=1).astype(bf16)
        r = inv[mine, :]
        coef = r * r * jnp.sum(gproj.astype(f32) * proj[mine, :], axis=1, keepdims=True) * (1.0 / width)

        @pl.loop(0, width // step)
        def _(n):
            cols = pl.ds(pl.multiple_of(n * step, step), step)
            gn = dot(gproj, w[cols, : 3 * hd], 1, 1)
            out = gin[:, cols].astype(f32) + r * (gn * gain[:, cols]) - x[mine, cols].astype(f32) * coef
            send[:, cols] = out.astype(bf16)


def flip(block, out):
    planes = out.shape[0]
    half = block.shape[1] // 2
    shard = half // planes
    pair = jnp.concatenate([block[:, :half], block[:, half:]], axis=0)
    turned = jnp.transpose(pair.astype(f32)).astype(bf16)
    for p in range(planes):
        out[p, :shard, :] = turned[p * shard : (p + 1) * shard, :]


def turn_early_half(gin, packed, out):
    tokens = gin.shape[0]
    out[:, out.shape[1] - packed.shape[1] :, :] = packed[...]
    flip(gin[tokens // 2 :, :], out)


def turn_late_half(flag, gin, recv, out):
    tokens = gin.shape[0]
    rows = recv.shape[0]
    first = jnp.where(flag[0] == 1, recv[...], gin[:rows, :])
    flip(jnp.concatenate([first, gin[rows : tokens // 2, :]], axis=0), out)


def spread(a, times):
    none = jnp.zeros_like(a)
    return [jnp.concatenate([none] * i + [a] + [none] * (times - 1 - i), axis=1) for i in range(times)]


def contract_early_half(got, att, out):
    planes, _, lanes = got.shape
    shard, two = out.shape
    hd = two // 2
    acc = jnp.zeros((shard, two), f32)
    old = jnp.zeros((shard // 2, 2 * two), f32)
    for p in range(0, planes, 2):
        pair = jnp.concatenate([got[p], got[p + 1]], axis=1)
        rhs = []
        far = []
        for b in (p, p + 1):
            rhs += spread(att[b, lanes // 2 : lanes, :], 2)
            far += spread(att[b, lanes:, :], 4)
        acc = acc + dot(pair[:shard], jnp.concatenate(rhs, axis=0))
        old = old + dot(pair[shard:], jnp.concatenate(far, axis=0))
    quarters = [old[:, i * hd : (i + 1) * hd] for i in range(4)]
    out[:, :hd] = acc[:, :hd] + jnp.concatenate(quarters[:2], axis=0)
    out[:, hd:] = acc[:, hd:] + jnp.concatenate(quarters[2:], axis=0)


def contract_late_half(got, att, sofar, out):
    planes, _, lanes = got.shape
    acc = sofar[...]
    for p in range(0, planes, 2):
        rhs = []
        for b in (p, p + 1):
            rhs += spread(att[b, : lanes // 2, :], 2)
        acc = acc + dot(jnp.concatenate([got[p], got[p + 1]], axis=1), jnp.concatenate(rhs, axis=0))
    out[...] = acc


def body(x_in, top_grad, norm_gain, proj_in, proj_out, key_cache, value_cache, prefix_len, early_out, early_dy):
    sections = lax.axis_size(SECTION)
    section = lax.axis_index(SECTION)
    zh = lax.axis_index("zh")
    planes = lax.axis_size(PLANE)
    x = x_in[0]
    tokens, width = x.shape
    kc = key_cache[0]
    vc = value_cache[0]
    crow, hd = kc.shape
    shard = width // (2 * planes)
    erows = early_dy.shape[1]
    swap = [(0, 1), (1, 0)]

    nx = lax.axis_size("x")
    ny = lax.axis_size("y")
    own = jnp.concatenate([proj_in[0], jnp.transpose(proj_out[0])], axis=1)
    other = lax.ppermute(own, "zh", swap)
    turns_x = [own]
    for d in range(1, nx):
        turns_x.append(lax.ppermute(own, "x", [(i, (i + d) % nx) for i in range(nx)]))
    wa = lax.all_gather(jnp.stack(turns_x)[None], "y", axis=0, tiled=True)
    along_y = lax.all_to_all(jnp.broadcast_to(other[None], (ny, *other.shape)), "y", 0, 0, tiled=True)
    wb = lax.all_to_all(jnp.broadcast_to(along_y[None], (nx, *along_y.shape)), "x", 0, 0, tiled=True)

    wide = x.astype(f32)
    gain = norm_gain.astype(f32)
    inv = lax.rsqrt(jnp.mean(wide * wide, axis=1, keepdims=True) + eps)
    normed = (wide * inv * gain).astype(bf16)

    packed = early_dy[0].reshape(erows, 2, planes, 2, shard // 2)
    packed = packed.transpose(2, 4, 1, 3, 0).reshape(planes, shard // 2, 4 * erows)

    shape = jax.ShapeDtypeStruct
    room = pltpu.CompilerParams(vmem_limit_bytes=24 << 20)
    w, q, kn, vn, pc, pn, proj, att = pl.pallas_call(
        forward_kernel,
        name="forward",
        in_specs=[SMEM, HBM, HBM, HBM, VMEM, VMEM, VMEM],
        out_specs=[VMEM] * 8,
        out_shape=[
            shape((2, ny, nx, shard, 4 * hd), bf16),
            shape((tokens, hd), bf16),
            shape((tokens, hd), bf16),
            shape((tokens, hd), bf16),
            shape((tokens, crow), f32),
            shape((tokens, tokens), f32),
            shape((tokens, 3 * hd), f32),
            shape((tokens + erows, hd), bf16),
        ],
        scratch_shapes=[
            pltpu.VMEM((tokens, width), bf16),
            pltpu.SemaphoreType.DMA((nx,)),
            pltpu.SemaphoreType.DMA((nx,)),
            pltpu.SemaphoreType.DMA,
        ],
        compiler_params=room,
    )(jnp.stack([prefix_len[0], lax.axis_index("x"), zh]), normed, wa, wb, kc, vc, early_out[0])
    w = near(w.reshape(width, 4 * hd))

    att_all = lax.all_gather(att[None], PLANE, axis=0, tiled=True)

    rows = tokens // PARTS
    stage = pl.pallas_call(
        stage_kernel,
        name="stage",
        in_specs=[SMEM] + [VMEM] * 18,
        out_specs=[VMEM] * 5,
        out_shape=[
            shape((rows, width), bf16),
            shape((tokens, hd), f32),
            shape((tokens, hd), f32),
            shape((tokens, crow), bf16),
            shape((tokens, hd), bf16),
        ],
        scratch_shapes=[pltpu.VMEM((rows, width), bf16)],
        input_output_aliases={15: 1, 16: 2, 17: 3, 18: 4},
        compiler_params=room,
    )
    is_top = section == sections - 1

    def place(t):
        part = sections - 1 - section + PARTS - 1 - t
        active = jnp.logical_and(part >= 0, part < PARTS)
        return jnp.clip(part, 0, PARTS - 1), active

    def keep(whole, piece, t, also):
        part, active = place(t)
        at = part * rows
        old = lax.dynamic_slice_in_dim(whole, at, rows, 0)
        return lax.dynamic_update_slice_in_dim(
            whole, jnp.where(jnp.logical_and(active, also), piece, old), at, 0
        )

    def compute(t, recv, state):
        part, active = place(t)
        flags = jnp.stack([active.astype(jnp.int32), part, is_top.astype(jnp.int32)])
        return stage(flags, recv, top_grad, w, x, gain, inv, q, kc, kn, vc, vn, pc, pn, proj, *state)

    recv = jnp.zeros((rows, width), bf16)
    gin_all = jnp.where(is_top, top_grad, jnp.zeros_like(top_grad))
    gx_all = jnp.zeros((tokens, width), bf16)
    state = (
        jnp.zeros((tokens, hd), f32),
        jnp.zeros((tokens, hd), f32),
        jnp.zeros((tokens, crow), bf16),
        jnp.zeros((tokens, hd), bf16),
    )
    turns = sections + PARTS - 1
    block = shape((planes, shard, tokens), bf16)
    down = [(i, i - 1) for i in range(1, sections)]

    halfway = sections + PARTS // 2 - 2
    for t in range(turns):
        if t == turns - 1:
            flag = (section == 0).astype(jnp.int32)[None]
            late = pl.pallas_call(
                turn_late_half,
                name="turn_late",
                in_specs=[SMEM, VMEM, VMEM],
                out_specs=VMEM,
                out_shape=block,
                compiler_params=room,
            )(flag, gin_all, recv)
            recv, late, got_soon = lax.optimization_barrier((recv, late, got_soon))
            got_late = lax.all_to_all(late, PLANE, 0, 0, tiled=True)
        elif t > 0:
            gin_all = keep(gin_all, recv, t, jnp.logical_not(is_top))
        send, *state = compute(t, recv, state)
        gx_all = keep(gx_all, send, t, True)
        if t == halfway:
            gin_now, _ = lax.optimization_barrier((gin_all, send))
            soon = pl.pallas_call(
                turn_early_half,
                name="turn_soon",
                in_specs=[VMEM, VMEM],
                out_specs=VMEM,
                out_shape=shape((planes, shard + shard // 2, tokens), bf16),
                compiler_params=room,
            )(gin_now, packed)
            got_soon = lax.all_to_all(soon, PLANE, 0, 0, tiled=True)
        if t < turns - 1:
            recv = lax.ppermute(send, SECTION, down)
    _, _, gsc, go_all = state
    key_out = dot(gsc, q, 0, 0).astype(bf16)
    value_out = dot(pc.astype(bf16), go_all, 0, 0).astype(bf16)

    def contract(kernel, *operands):
        return pl.pallas_call(
            kernel,
            in_specs=[VMEM] * len(operands),
            out_specs=VMEM,
            out_shape=shape((shard, 2 * hd), f32),
            compiler_params=room,
        )(*operands)

    whole = contract(contract_late_half, got_late, att_all, contract(contract_early_half, got_soon, att_all))
    first, second = whole[:, :hd], whole[:, hd:]
    away = lax.ppermute(jnp.where(zh == 0, second, first), "zh", swap)
    wo = jnp.transpose(jnp.where(zh == 0, first, second) + away)
    return gx_all[None], key_out[None], value_out[None], wo[None]


def solution(mesh):
    ny, nx = (8, 4) if mesh.shape["dp"] == 64 else (2, mesh.shape["dp"] // 4)
    fine = Mesh(mesh.devices.reshape(mesh.shape["section"] // 2, 2, 2, ny, nx), ("zl", "core", "zh", "y", "x"))
    in_specs = (
        P(SECTION, DP, None),
        P(DP, None),
        P(SECTION, None),
        P(SECTION, DP, None),
        P(SECTION, None, DP),
        P(SECTION, DP, None),
        P(SECTION, DP, None),
        P(DP),
        P(SECTION, DP, None),
        P(SECTION, DP, None),
    )
    out_specs = (
        P(SECTION, DP, None),
        P(SECTION, DP, None),
        P(SECTION, DP, None),
        P(SECTION, None, DP),
    )
    return jax.shard_map(body, mesh=fine, in_specs=in_specs, out_specs=out_specs, check_vma=False)
```

```python
import jax
import jax.numpy as jnp
from jax import lax
from jax.experimental import pallas as pl
from jax.experimental.pallas import tpu as pltpu
from jax.sharding import Mesh
from jax.sharding import PartitionSpec as P


eps = 1e-06
bf16 = jnp.bfloat16
f32 = jnp.float32
PARTS = 4
SECTION = ("zl", "core")
PLANE = ("y", "x")
DP = ("zh", "y", "x")
VMEM = pl.BlockSpec(memory_space=pltpu.VMEM)
HBM = pl.BlockSpec(memory_space=pltpu.HBM)
SMEM = pl.BlockSpec(memory_space=pltpu.SMEM)


def dot(a, b, ca=1, cb=0):
    return lax.dot_general(a, b, (((ca,), (cb,)), ((), ())), preferred_element_type=f32)


def near(a):
    return pltpu.with_memory_space_constraint(a, pltpu.VMEM)


def far(a):
    return pltpu.with_memory_space_constraint(a, pltpu.HBM)


def chunk_of(width):
    return 640 if width % 640 == 0 else width


def forward_kernel(
    place, normed_hbm, wa, wb, kc, vc, eo, w, q_ref, kn_ref, vn_ref, pc_ref, pn_ref, proj_ref, att_ref,
    normed, sem_a, sem_b, sem_n,
):
    len_ref = place
    hd = kc.shape[1]
    rows, width = normed.shape
    nx, ny, shard, _ = wb.shape
    half = width // 2
    zh = place[2]
    take_a = [
        pltpu.make_async_copy(wa.at[:, lax.rem(place[1] - j + nx, nx)], w.at[zh, :, j], sem_a.at[j]) for j in range(nx)
    ]
    take_b = [pltpu.make_async_copy(wb.at[j], w.at[1 - zh, :, j], sem_b.at[j]) for j in range(nx)]
    take_n = pltpu.make_async_copy(normed_hbm, normed, sem_n)
    take_n.start()
    for copy in take_a + take_b:
        copy.start()
    take_n.wait()
    acc = jnp.zeros((rows, 3 * hd), f32)
    deep = max(1, ny // 4)
    step = deep * nx * shard
    for h, copies in ((zh, take_a), (1 - zh, take_b)):
        for copy in copies:
            copy.wait()
        for c in range(0, ny, deep):
            cols = pl.ds(pl.multiple_of(h * half + c * nx * shard, 128), step)
            acc = acc + dot(normed[:, cols], w[h, c : c + deep, :, :, : 3 * hd].reshape(step, 3 * hd))
    proj_ref[...] = acc
    low = acc.astype(bf16)
    q = low[:, :hd]
    kn = low[:, hd : 2 * hd]
    vn = low[:, 2 * hd :]
    q_ref[...] = q
    kn_ref[...] = kn
    vn_ref[...] = vn
    scale = hd ** (-0.5)
    sc = dot(q, kc[...], 1, 1) * scale
    sn = dot(q, kn, 1, 1) * scale
    see_c = lax.broadcasted_iota(jnp.int32, sc.shape, 1) < len_ref[0]
    see_n = lax.broadcasted_iota(jnp.int32, sn.shape, 1) <= lax.broadcasted_iota(jnp.int32, sn.shape, 0)
    sc = jnp.where(see_c, sc, -jnp.inf)
    sn = jnp.where(see_n, sn, -jnp.inf)
    top = jnp.maximum(jnp.max(sc, axis=1, keepdims=True), jnp.max(sn, axis=1, keepdims=True))
    wc = jnp.where(see_c, jnp.exp(sc - top), 0.0)
    wn = jnp.where(see_n, jnp.exp(sn - top), 0.0)
    total = jnp.sum(wc, axis=1, keepdims=True) + jnp.sum(wn, axis=1, keepdims=True)
    pc = wc / total
    pn = wn / total
    pc_ref[...] = pc
    pn_ref[...] = pn
    att_ref[:rows, :] = (dot(pc.astype(bf16), vc[...]) + dot(pn.astype(bf16), vn)).astype(bf16)
    att_ref[rows:, :] = eo[...]


def stage_kernel(
    flags, recv, top, w, x, gain, inv, q, kc, kn, vc, vn, pc, pn, proj, gkn_in, gvn_in, gsc_in, go_in,
    send, gkn, gvn, gsc, go_all, gin,
):
    rows = send.shape[0]
    hd = q.shape[1]
    width = w.shape[0]
    step = chunk_of(width // 2)
    scale = hd ** (-0.5)
    active = flags[0] == 1
    r0 = pl.multiple_of(flags[1] * rows, rows)
    is_top = flags[2] == 1
    mine = pl.ds(r0, rows)
    pieces = [slice(c, c + step) for c in range(0, width, step)]

    gkn[...] = gkn_in[...]
    gvn[...] = gvn_in[...]
    gsc[...] = gsc_in[...]
    go_all[...] = go_in[...]

    @pl.when(jnp.logical_and(active, is_top))
    def _():
        gin[...] = top[mine, :]

    @pl.when(jnp.logical_and(active, jnp.logical_not(is_top)))
    def _():
        gin[...] = recv[...]

    @pl.when(active)
    def _():
        acc = jnp.zeros((rows, hd), f32)
        for cols in pieces:
            acc = acc + dot(gin[:, cols], w[cols, 3 * hd :])
        go = acc.astype(bf16)
        go_all[mine, :] = go
        prob_c = pc[mine, :]
        prob_n = pn[mine, :]
        gp_c = dot(go, vc[...], 1, 1)
        gp_n = dot(go, vn[...], 1, 1)
        delta = jnp.sum(prob_c * gp_c, axis=1, keepdims=True) + jnp.sum(prob_n * gp_n, axis=1, keepdims=True)
        gs_c = (prob_c * (gp_c - delta) * scale).astype(bf16)
        gs_n = (prob_n * (gp_n - delta) * scale).astype(bf16)
        gsc[mine, :] = gs_c
        gq = dot(gs_c, kc[...]) + dot(gs_n, kn[...])
        gkn[...] += dot(gs_n, q[mine, :], 0, 0)
        gvn[...] += dot(prob_n.astype(bf16), go, 0, 0)
        gproj = jnp.concatenate([gq, gkn[mine, :], gvn[mine, :]], axis=1).astype(bf16)
        r = inv[mine, :]
        coef = r * r * jnp.sum(gproj.astype(f32) * proj[mine, :], axis=1, keepdims=True) * (1.0 / width)

        @pl.loop(0, width // step)
        def _(n):
            cols = pl.ds(pl.multiple_of(n * step, step), step)
            gn = dot(gproj, w[cols, : 3 * hd], 1, 1)
            out = gin[:, cols].astype(f32) + r * (gn * gain[:, cols]) - x[mine, cols].astype(f32) * coef
            send[:, cols] = out.astype(bf16)


def flip(block, out):
    planes = out.shape[0]
    half = block.shape[1] // 2
    shard = half // planes
    pair = jnp.concatenate([block[:, :half], block[:, half:]], axis=0)
    turned = jnp.transpose(pair.astype(f32)).astype(bf16)
    for p in range(planes):
        out[p, :shard, :] = turned[p * shard : (p + 1) * shard, :]


def turn_early_half(gin, packed, out):
    tokens = gin.shape[0]
    out[:, out.shape[1] - packed.shape[1] :, :] = packed[...]
    flip(gin[tokens // 2 :, :], out)


def turn_late_half(flag, gin, recv, out):
    tokens = gin.shape[0]
    rows = recv.shape[0]
    first = jnp.where(flag[0] == 1, recv[...], gin[:rows, :])
    flip(jnp.concatenate([first, gin[rows : tokens // 2, :]], axis=0), out)


def spread(a, times):
    none = jnp.zeros_like(a)
    return [jnp.concatenate([none] * i + [a] + [none] * (times - 1 - i), axis=1) for i in range(times)]


def contract_early_half(got, att, out):
    planes, _, lanes = got.shape
    shard, two = out.shape
    hd = two // 2
    acc = jnp.zeros((shard, two), f32)
    old = jnp.zeros((shard // 2, 2 * two), f32)
    for p in range(0, planes, 2):
        pair = jnp.concatenate([got[p], got[p + 1]], axis=1)
        rhs = []
        far = []
        for b in (p, p + 1):
            rhs += spread(att[b, lanes // 2 : lanes, :], 2)
            far += spread(att[b, lanes:, :], 4)
        acc = acc + dot(pair[:shard], jnp.concatenate(rhs, axis=0))
        old = old + dot(pair[shard:], jnp.concatenate(far, axis=0))
    quarters = [old[:, i * hd : (i + 1) * hd] for i in range(4)]
    out[:, :hd] = acc[:, :hd] + jnp.concatenate(quarters[:2], axis=0)
    out[:, hd:] = acc[:, hd:] + jnp.concatenate(quarters[2:], axis=0)


def contract_late_half(got, att, sofar, out):
    planes, _, lanes = got.shape
    acc = sofar[...]
    for p in range(0, planes, 2):
        rhs = []
        for b in (p, p + 1):
            rhs += spread(att[b, : lanes // 2, :], 2)
        acc = acc + dot(jnp.concatenate([got[p], got[p + 1]], axis=1), jnp.concatenate(rhs, axis=0))
    out[...] = acc


def body(x_in, top_grad, norm_gain, proj_in, proj_out, key_cache, value_cache, prefix_len, early_out, early_dy):
    sections = lax.axis_size(SECTION)
    section = lax.axis_index(SECTION)
    zh = lax.axis_index("zh")
    planes = lax.axis_size(PLANE)
    x = x_in[0]
    tokens, width = x.shape
    kc = key_cache[0]
    vc = value_cache[0]
    crow, hd = kc.shape
    shard = width // (2 * planes)
    erows = early_dy.shape[1]
    swap = [(0, 1), (1, 0)]

    nx = lax.axis_size("x")
    ny = lax.axis_size("y")
    own = jnp.concatenate([proj_in[0], jnp.transpose(proj_out[0])], axis=1)
    other = lax.ppermute(own, "zh", swap)
    turns_x = [own]
    for d in range(1, nx):
        turns_x.append(lax.ppermute(own, "x", [(i, (i + d) % nx) for i in range(nx)]))
    along_y = lax.all_to_all(jnp.broadcast_to(other[None], (ny, *other.shape)), "y", 0, 0, tiled=True)
    mine, along_y, early_dy = lax.optimization_barrier((jnp.stack(turns_x)[None], along_y, early_dy))
    wa = lax.all_gather(mine, "y", axis=0, tiled=True)
    wb = lax.all_to_all(jnp.broadcast_to(along_y[None], (nx, *along_y.shape)), "x", 0, 0, tiled=True)

    wide = x.astype(f32)
    gain = norm_gain.astype(f32)
    inv = lax.rsqrt(jnp.mean(wide * wide, axis=1, keepdims=True) + eps)
    normed = (wide * inv * gain).astype(bf16)

    packed = early_dy[0].reshape(erows, 2, planes, 2, shard // 2)
    packed = packed.transpose(2, 4, 1, 3, 0).reshape(planes, shard // 2, 4 * erows)

    shape = jax.ShapeDtypeStruct
    room = pltpu.CompilerParams(vmem_limit_bytes=24 << 20)
    w, q, kn, vn, pc, pn, proj, att = pl.pallas_call(
        forward_kernel,
        name="forward",
        in_specs=[SMEM, HBM, HBM, HBM, VMEM, VMEM, VMEM],
        out_specs=[VMEM] * 8,
        out_shape=[
            shape((2, ny, nx, shard, 4 * hd), bf16),
            shape((tokens, hd), bf16),
            shape((tokens, hd), bf16),
            shape((tokens, hd), bf16),
            shape((tokens, crow), f32),
            shape((tokens, tokens), f32),
            shape((tokens, 3 * hd), f32),
            shape((tokens + erows, hd), bf16),
        ],
        scratch_shapes=[
            pltpu.VMEM((tokens, width), bf16),
            pltpu.SemaphoreType.DMA((nx,)),
            pltpu.SemaphoreType.DMA((nx,)),
            pltpu.SemaphoreType.DMA,
        ],
        compiler_params=room,
    )(jnp.stack([prefix_len[0], lax.axis_index("x"), zh]), far(normed), far(wa), far(wb), kc, vc, early_out[0])
    w = near(w.reshape(width, 4 * hd))

    att_all = lax.all_gather(att[None], PLANE, axis=0, tiled=True)

    rows = tokens // PARTS
    stage = pl.pallas_call(
        stage_kernel,
        name="stage",
        in_specs=[SMEM] + [VMEM] * 18,
        out_specs=[VMEM] * 5,
        out_shape=[
            shape((rows, width), bf16),
            shape((tokens, hd), f32),
            shape((tokens, hd), f32),
            shape((tokens, crow), bf16),
            shape((tokens, hd), bf16),
        ],
        scratch_shapes=[pltpu.VMEM((rows, width), bf16)],
        input_output_aliases={15: 1, 16: 2, 17: 3, 18: 4},
        compiler_params=room,
    )
    is_top = section == sections - 1

    def place(t):
        part = sections - 1 - section + PARTS - 1 - t
        active = jnp.logical_and(part >= 0, part < PARTS)
        return jnp.clip(part, 0, PARTS - 1), active

    def keep(whole, piece, t, also):
        part, active = place(t)
        at = part * rows
        old = lax.dynamic_slice_in_dim(whole, at, rows, 0)
        return lax.dynamic_update_slice_in_dim(
            whole, jnp.where(jnp.logical_and(active, also), piece, old), at, 0
        )

    def compute(t, recv, state):
        part, active = place(t)
        flags = jnp.stack([active.astype(jnp.int32), part, is_top.astype(jnp.int32)])
        return stage(flags, recv, top_grad, w, x, gain, inv, q, kc, kn, vc, vn, pc, pn, proj, *state)

    recv = jnp.zeros((rows, width), bf16)
    gin_all = jnp.where(is_top, top_grad, jnp.zeros_like(top_grad))
    gx_all = jnp.zeros((tokens, width), bf16)
    state = (
        jnp.zeros((tokens, hd), f32),
        jnp.zeros((tokens, hd), f32),
        jnp.zeros((tokens, crow), bf16),
        jnp.zeros((tokens, hd), bf16),
    )
    turns = sections + PARTS - 1
    block = shape((planes, shard, tokens), bf16)
    down = [(i, i - 1) for i in range(1, sections)]

    halfway = sections + PARTS // 2 - 2
    for t in range(turns):
        if t == turns - 1:
            flag = (section == 0).astype(jnp.int32)[None]
            late = pl.pallas_call(
                turn_late_half,
                name="turn_late",
                in_specs=[SMEM, VMEM, VMEM],
                out_specs=VMEM,
                out_shape=block,
                compiler_params=room,
            )(flag, gin_all, recv)
            recv, late, got_soon = lax.optimization_barrier((recv, late, got_soon))
            got_late = lax.all_to_all(late, PLANE, 0, 0, tiled=True)
        elif t > 0:
            gin_all = keep(gin_all, recv, t, jnp.logical_not(is_top))
        send, *state = compute(t, recv, state)
        gx_all = keep(gx_all, send, t, True)
        if t == halfway:
            gin_now, _ = lax.optimization_barrier((gin_all, send))
            soon = pl.pallas_call(
                turn_early_half,
                name="turn_soon",
                in_specs=[VMEM, VMEM],
                out_specs=VMEM,
                out_shape=shape((planes, shard + shard // 2, tokens), bf16),
                compiler_params=room,
            )(gin_now, packed)
            got_soon = lax.all_to_all(soon, PLANE, 0, 0, tiled=True)
        if t < turns - 1:
            recv = lax.ppermute(send, SECTION, down)
    _, _, gsc, go_all = state
    key_out = dot(gsc, q, 0, 0).astype(bf16)
    value_out = dot(pc.astype(bf16), go_all, 0, 0).astype(bf16)

    def contract(kernel, *operands):
        return pl.pallas_call(
            kernel,
            in_specs=[VMEM] * len(operands),
            out_specs=VMEM,
            out_shape=shape((shard, 2 * hd), f32),
            compiler_params=room,
        )(*operands)

    whole = contract(contract_late_half, got_late, att_all, contract(contract_early_half, got_soon, att_all))
    first, second = whole[:, :hd], whole[:, hd:]
    away = lax.ppermute(jnp.where(zh == 0, second, first), "zh", swap)
    wo = jnp.transpose(jnp.where(zh == 0, first, second) + away)
    return gx_all[None], key_out[None], value_out[None], wo[None]


def solution(mesh):
    ny, nx = (8, 4) if mesh.shape["dp"] == 64 else (2, mesh.shape["dp"] // 4)
    fine = Mesh(mesh.devices.reshape(mesh.shape["section"] // 2, 2, 2, ny, nx), ("zl", "core", "zh", "y", "x"))
    in_specs = (
        P(SECTION, DP, None),
        P(DP, None),
        P(SECTION, None),
        P(SECTION, DP, None),
        P(SECTION, None, DP),
        P(SECTION, DP, None),
        P(SECTION, DP, None),
        P(DP),
        P(SECTION, DP, None),
        P(SECTION, DP, None),
    )
    out_specs = (
        P(SECTION, DP, None),
        P(SECTION, DP, None),
        P(SECTION, DP, None),
        P(SECTION, None, DP),
    )
    return jax.shard_map(body, mesh=fine, in_specs=in_specs, out_specs=out_specs, check_vma=False)
```

```python
import jax
import jax.numpy as jnp
from jax import lax
from jax.experimental import pallas as pl
from jax.experimental.pallas import tpu as pltpu
from jax.sharding import Mesh
from jax.sharding import PartitionSpec as P


eps = 1e-06
bf16 = jnp.bfloat16
f32 = jnp.float32
PARTS = 4
SECTION = ("zl", "core")
PLANE = ("y", "x")
DP = ("zh", "y", "x")
VMEM = pl.BlockSpec(memory_space=pltpu.VMEM)
HBM = pl.BlockSpec(memory_space=pltpu.HBM)
SMEM = pl.BlockSpec(memory_space=pltpu.SMEM)


def dot(a, b, ca=1, cb=0):
    return lax.dot_general(a, b, (((ca,), (cb,)), ((), ())), preferred_element_type=f32)


def near(a):
    return pltpu.with_memory_space_constraint(a, pltpu.VMEM)


def far(a):
    return pltpu.with_memory_space_constraint(a, pltpu.HBM)


def chunk_of(width):
    return 640 if width % 640 == 0 else width


def forward_kernel(
    place, normed_hbm, wa, wb, kc, vc, eo, w, q_ref, kn_ref, vn_ref, pc_ref, pn_ref, proj_ref, att_ref,
    normed, sem_a, sem_b, sem_n,
):
    len_ref = place
    hd = kc.shape[1]
    rows, width = normed.shape
    nx, ny, shard, _ = wb.shape
    half = width // 2
    zh = place[2]
    take_a = [
        pltpu.make_async_copy(wa.at[:, lax.rem(place[1] - j + nx, nx)], w.at[zh, :, j], sem_a.at[j]) for j in range(nx)
    ]
    take_b = [pltpu.make_async_copy(wb.at[j], w.at[1 - zh, :, j], sem_b.at[j]) for j in range(nx)]
    take_n = pltpu.make_async_copy(normed_hbm, normed, sem_n)
    take_n.start()
    for copy in take_a + take_b:
        copy.start()
    take_n.wait()
    acc = jnp.zeros((rows, 3 * hd), f32)
    deep = max(1, ny // 4)
    step = deep * nx * shard
    for h, copies in ((zh, take_a), (1 - zh, take_b)):
        for copy in copies:
            copy.wait()
        for c in range(0, ny, deep):
            cols = pl.ds(pl.multiple_of(h * half + c * nx * shard, 128), step)
            acc = acc + dot(normed[:, cols], w[h, c : c + deep, :, :, : 3 * hd].reshape(step, 3 * hd))
    proj_ref[...] = acc
    low = acc.astype(bf16)
    q = low[:, :hd]
    kn = low[:, hd : 2 * hd]
    vn = low[:, 2 * hd :]
    q_ref[...] = q
    kn_ref[...] = kn
    vn_ref[...] = vn
    scale = hd ** (-0.5)
    sc = dot(q, kc[...], 1, 1) * scale
    sn = dot(q, kn, 1, 1) * scale
    see_c = lax.broadcasted_iota(jnp.int32, sc.shape, 1) < len_ref[0]
    see_n = lax.broadcasted_iota(jnp.int32, sn.shape, 1) <= lax.broadcasted_iota(jnp.int32, sn.shape, 0)
    sc = jnp.where(see_c, sc, -jnp.inf)
    sn = jnp.where(see_n, sn, -jnp.inf)
    top = jnp.maximum(jnp.max(sc, axis=1, keepdims=True), jnp.max(sn, axis=1, keepdims=True))
    wc = jnp.where(see_c, jnp.exp(sc - top), 0.0)
    wn = jnp.where(see_n, jnp.exp(sn - top), 0.0)
    total = jnp.sum(wc, axis=1, keepdims=True) + jnp.sum(wn, axis=1, keepdims=True)
    pc = wc / total
    pn = wn / total
    pc_ref[...] = pc
    pn_ref[...] = pn
    att_ref[:rows, :] = (dot(pc.astype(bf16), vc[...]) + dot(pn.astype(bf16), vn)).astype(bf16)
    att_ref[rows:, :] = eo[...]


def stage_kernel(
    flags, recv, top, w, x, gain, inv, q, kc, kn, vc, vn, pc, pn, proj, gkn_in, gvn_in, gsc_in, go_in,
    send, gkn, gvn, gsc, go_all, gin,
):
    rows = send.shape[0]
    hd = q.shape[1]
    width = w.shape[0]
    step = chunk_of(width // 2)
    scale = hd ** (-0.5)
    active = flags[0] == 1
    r0 = pl.multiple_of(flags[1] * rows, rows)
    is_top = flags[2] == 1
    mine = pl.ds(r0, rows)
    pieces = [slice(c, c + step) for c in range(0, width, step)]

    gkn[...] = gkn_in[...]
    gvn[...] = gvn_in[...]
    gsc[...] = gsc_in[...]
    go_all[...] = go_in[...]

    @pl.when(jnp.logical_and(active, is_top))
    def _():
        gin[...] = top[mine, :]

    @pl.when(jnp.logical_and(active, jnp.logical_not(is_top)))
    def _():
        gin[...] = recv[...]

    @pl.when(active)
    def _():
        acc = jnp.zeros((rows, hd), f32)
        for cols in pieces:
            acc = acc + dot(gin[:, cols], w[cols, 3 * hd :])
        go = acc.astype(bf16)
        go_all[mine, :] = go
        prob_c = pc[mine, :]
        prob_n = pn[mine, :]
        gp_c = dot(go, vc[...], 1, 1)
        gp_n = dot(go, vn[...], 1, 1)
        delta = jnp.sum(prob_c * gp_c, axis=1, keepdims=True) + jnp.sum(prob_n * gp_n, axis=1, keepdims=True)
        gs_c = (prob_c * (gp_c - delta) * scale).astype(bf16)
        gs_n = (prob_n * (gp_n - delta) * scale).astype(bf16)
        gsc[mine, :] = gs_c
        gq = dot(gs_c, kc[...]) + dot(gs_n, kn[...])
        gkn[...] += dot(gs_n, q[mine, :], 0, 0)
        gvn[...] += dot(prob_n.astype(bf16), go, 0, 0)
        gproj = jnp.concatenate([gq, gkn[mine, :], gvn[mine, :]], axis=1).astype(bf16)
        r = inv[mine, :]
        coef = r * r * jnp.sum(gproj.astype(f32) * proj[mine, :], axis=1, keepdims=True) * (1.0 / width)

        @pl.loop(0, width // step)
        def _(n):
            cols = pl.ds(pl.multiple_of(n * step, step), step)
            gn = dot(gproj, w[cols, : 3 * hd], 1, 1)
            out = gin[:, cols].astype(f32) + r * (gn * gain[:, cols]) - x[mine, cols].astype(f32) * coef
            send[:, cols] = out.astype(bf16)


def flip(block, out):
    planes = out.shape[0]
    half = block.shape[1] // 2
    shard = half // planes
    pair = jnp.concatenate([block[:, :half], block[:, half:]], axis=0)
    turned = jnp.transpose(pair.astype(f32)).astype(bf16)
    for p in range(planes):
        out[p, :shard, :] = turned[p * shard : (p + 1) * shard, :]


def turn_early_half(gin, packed, out):
    tokens = gin.shape[0]
    out[:, out.shape[1] - packed.shape[1] :, :] = packed[...]
    flip(gin[tokens // 2 :, :], out)


def turn_late_half(flag, gin, recv, out):
    tokens = gin.shape[0]
    rows = recv.shape[0]
    first = jnp.where(flag[0] == 1, recv[...], gin[:rows, :])
    flip(jnp.concatenate([first, gin[rows : tokens // 2, :]], axis=0), out)


def finish_kernel(flags, kept, soon, last, out):
    rows = soon.shape[0]
    out[...] = kept[...]

    @pl.when(flags[0] == 1)
    def _():
        out[pl.ds(pl.multiple_of(flags[1] * rows, rows), rows), :] = soon[...]

    @pl.when(flags[2] == 1)
    def _():
        out[pl.ds(pl.multiple_of(flags[3] * rows, rows), rows), :] = last[...]


def spread(a, times):
    none = jnp.zeros_like(a)
    return [jnp.concatenate([none] * i + [a] + [none] * (times - 1 - i), axis=1) for i in range(times)]


def contract_early_half(got, att, out):
    planes, _, lanes = got.shape
    shard, two = out.shape
    hd = two // 2
    acc = jnp.zeros((shard, two), f32)
    old = jnp.zeros((shard // 2, 2 * two), f32)
    for p in range(0, planes, 2):
        pair = jnp.concatenate([got[p], got[p + 1]], axis=1)
        rhs = []
        far = []
        for b in (p, p + 1):
            rhs += spread(att[b, lanes // 2 : lanes, :], 2)
            far += spread(att[b, lanes:, :], 4)
        acc = acc + dot(pair[:shard], jnp.concatenate(rhs, axis=0))
        old = old + dot(pair[shard:], jnp.concatenate(far, axis=0))
    quarters = [old[:, i * hd : (i + 1) * hd] for i in range(4)]
    out[:, :hd] = acc[:, :hd] + jnp.concatenate(quarters[:2], axis=0)
    out[:, hd:] = acc[:, hd:] + jnp.concatenate(quarters[2:], axis=0)


def contract_late_half(got, att, sofar, out):
    planes, _, lanes = got.shape
    acc = sofar[...]
    for p in range(0, planes, 2):
        rhs = []
        for b in (p, p + 1):
            rhs += spread(att[b, : lanes // 2, :], 2)
        acc = acc + dot(jnp.concatenate([got[p], got[p + 1]], axis=1), jnp.concatenate(rhs, axis=0))
    out[...] = acc


def body(x_in, top_grad, norm_gain, proj_in, proj_out, key_cache, value_cache, prefix_len, early_out, early_dy):
    sections = lax.axis_size(SECTION)
    section = lax.axis_index(SECTION)
    zh = lax.axis_index("zh")
    planes = lax.axis_size(PLANE)
    x = x_in[0]
    tokens, width = x.shape
    kc = key_cache[0]
    vc = value_cache[0]
    crow, hd = kc.shape
    shard = width // (2 * planes)
    erows = early_dy.shape[1]
    swap = [(0, 1), (1, 0)]

    nx = lax.axis_size("x")
    ny = lax.axis_size("y")
    own = jnp.concatenate([proj_in[0], jnp.transpose(proj_out[0])], axis=1)
    other = lax.ppermute(own, "zh", swap)
    turns_x = [own]
    for d in range(1, nx):
        turns_x.append(lax.ppermute(own, "x", [(i, (i + d) % nx) for i in range(nx)]))
    along_y = lax.all_to_all(jnp.broadcast_to(other[None], (ny, *other.shape)), "y", 0, 0, tiled=True)
    mine = jnp.stack(turns_x)[None]
    along_y, early_dy = lax.optimization_barrier((along_y, early_dy))
    wa = lax.all_gather(mine, "y", axis=0, tiled=True)
    copies, x = lax.optimization_barrier((jnp.broadcast_to(along_y[None], (nx, *along_y.shape)), x))
    wb = lax.all_to_all(copies, "x", 0, 0, tiled=True)

    wide = x.astype(f32)
    gain = norm_gain.astype(f32)
    inv = lax.rsqrt(jnp.mean(wide * wide, axis=1, keepdims=True) + eps)
    normed = (wide * inv * gain).astype(bf16)

    packed = early_dy[0].reshape(erows, 2, planes, 2, shard // 2)
    packed = packed.transpose(2, 4, 1, 3, 0).reshape(planes, shard // 2, 4 * erows)

    shape = jax.ShapeDtypeStruct
    room = pltpu.CompilerParams(vmem_limit_bytes=24 << 20)
    w, q, kn, vn, pc, pn, proj, att = pl.pallas_call(
        forward_kernel,
        name="forward",
        in_specs=[SMEM, HBM, HBM, HBM, VMEM, VMEM, VMEM],
        out_specs=[VMEM] * 8,
        out_shape=[
            shape((2, ny, nx, shard, 4 * hd), bf16),
            shape((tokens, hd), bf16),
            shape((tokens, hd), bf16),
            shape((tokens, hd), bf16),
            shape((tokens, crow), f32),
            shape((tokens, tokens), f32),
            shape((tokens, 3 * hd), f32),
            shape((tokens + erows, hd), bf16),
        ],
        scratch_shapes=[
            pltpu.VMEM((tokens, width), bf16),
            pltpu.SemaphoreType.DMA((nx,)),
            pltpu.SemaphoreType.DMA((nx,)),
            pltpu.SemaphoreType.DMA,
        ],
        compiler_params=room,
    )(jnp.stack([prefix_len[0], lax.axis_index("x"), zh]), far(normed), far(wa), far(wb), kc, vc, early_out[0])
    w = near(w.reshape(width, 4 * hd))

    att_all = lax.all_gather(att[None], PLANE, axis=0, tiled=True)

    rows = tokens // PARTS
    stage = pl.pallas_call(
        stage_kernel,
        name="stage",
        in_specs=[SMEM] + [VMEM] * 18,
        out_specs=[VMEM] * 5,
        out_shape=[
            shape((rows, width), bf16),
            shape((tokens, hd), f32),
            shape((tokens, hd), f32),
            shape((tokens, crow), bf16),
            shape((tokens, hd), bf16),
        ],
        scratch_shapes=[pltpu.VMEM((rows, width), bf16)],
        input_output_aliases={15: 1, 16: 2, 17: 3, 18: 4},
        compiler_params=room,
    )
    is_top = section == sections - 1

    def place(t):
        part = sections - 1 - section + PARTS - 1 - t
        active = jnp.logical_and(part >= 0, part < PARTS)
        return jnp.clip(part, 0, PARTS - 1), active

    def keep(whole, piece, t, also):
        part, active = place(t)
        at = part * rows
        old = lax.dynamic_slice_in_dim(whole, at, rows, 0)
        return lax.dynamic_update_slice_in_dim(
            whole, jnp.where(jnp.logical_and(active, also), piece, old), at, 0
        )

    def compute(t, recv, state):
        part, active = place(t)
        flags = jnp.stack([active.astype(jnp.int32), part, is_top.astype(jnp.int32)])
        return stage(flags, recv, top_grad, w, x, gain, inv, q, kc, kn, vc, vn, pc, pn, proj, *state)

    recv = jnp.zeros((rows, width), bf16)
    gin_all = jnp.where(is_top, top_grad, jnp.zeros_like(top_grad))
    gx_all = jnp.zeros((tokens, width), bf16)
    state = (
        jnp.zeros((tokens, hd), f32),
        jnp.zeros((tokens, hd), f32),
        jnp.zeros((tokens, crow), bf16),
        jnp.zeros((tokens, hd), bf16),
    )
    turns = sections + PARTS - 1
    block = shape((planes, shard, tokens), bf16)
    down = [(i, i - 1) for i in range(1, sections)]

    halfway = sections + PARTS // 2 - 2
    for t in range(turns):
        if t == turns - 1:
            recv, gx_all = lax.optimization_barrier((recv, gx_all))
            flag = (section == 0).astype(jnp.int32)[None]
            late = pl.pallas_call(
                turn_late_half,
                name="turn_late",
                in_specs=[SMEM, VMEM, VMEM],
                out_specs=VMEM,
                out_shape=block,
                compiler_params=room,
            )(flag, gin_all, recv)
            recv, late, got_soon = lax.optimization_barrier((recv, late, got_soon))
            got_late = lax.all_to_all(late, PLANE, 0, 0, tiled=True)
        elif t > 0:
            gin_all = keep(gin_all, recv, t, jnp.logical_not(is_top))
        send, *state = compute(t, recv, state)
        if t < turns - 2:
            gx_all = keep(gx_all, send, t, True)
        elif t == turns - 2:
            sent = send
        if t == halfway:
            gin_now, _ = lax.optimization_barrier((gin_all, send))
            soon = pl.pallas_call(
                turn_early_half,
                name="turn_soon",
                in_specs=[VMEM, VMEM],
                out_specs=VMEM,
                out_shape=shape((planes, shard + shard // 2, tokens), bf16),
                compiler_params=room,
            )(gin_now, packed)
            got_soon = lax.all_to_all(soon, PLANE, 0, 0, tiled=True)
        if t < turns - 1:
            recv = lax.ppermute(send, SECTION, down)
    (part_soon, on_soon), (part_last, on_last) = place(turns - 2), place(turns - 1)
    flags = [on_soon.astype(jnp.int32), part_soon, on_last.astype(jnp.int32), part_last]
    gx_all = pl.pallas_call(
        finish_kernel,
        name="finish",
        in_specs=[SMEM] + [VMEM] * 3,
        out_specs=VMEM,
        out_shape=shape((tokens, width), bf16),
        compiler_params=room,
    )(jnp.stack(flags), gx_all, sent, send)
    _, _, gsc, go_all = state
    key_out = dot(gsc, q, 0, 0).astype(bf16)
    value_out = dot(pc.astype(bf16), go_all, 0, 0).astype(bf16)

    def contract(kernel, *operands):
        return pl.pallas_call(
            kernel,
            in_specs=[VMEM] * len(operands),
            out_specs=VMEM,
            out_shape=shape((shard, 2 * hd), f32),
            compiler_params=room,
        )(*operands)

    whole = contract(contract_late_half, got_late, att_all, contract(contract_early_half, got_soon, att_all))
    first, second = whole[:, :hd], whole[:, hd:]
    away = lax.ppermute(jnp.where(zh == 0, second, first), "zh", swap)
    wo = jnp.transpose(jnp.where(zh == 0, first, second) + away)
    return gx_all[None], key_out[None], value_out[None], wo[None]


def solution(mesh):
    ny, nx = (8, 4) if mesh.shape["dp"] == 64 else (2, mesh.shape["dp"] // 4)
    fine = Mesh(mesh.devices.reshape(mesh.shape["section"] // 2, 2, 2, ny, nx), ("zl", "core", "zh", "y", "x"))
    in_specs = (
        P(SECTION, DP, None),
        P(DP, None),
        P(SECTION, None),
        P(SECTION, DP, None),
        P(SECTION, None, DP),
        P(SECTION, DP, None),
        P(SECTION, DP, None),
        P(DP),
        P(SECTION, DP, None),
        P(SECTION, DP, None),
    )
    out_specs = (
        P(SECTION, DP, None),
        P(SECTION, DP, None),
        P(SECTION, DP, None),
        P(SECTION, None, DP),
    )
    return jax.shard_map(body, mesh=fine, in_specs=in_specs, out_specs=out_specs, check_vma=False)
```
